32 devices in a mesh: groups: 2 (over y), date: 4 (over z), row: 2 (over core), col: 2 (over x).
Axes of the slice: x: 2, y: 2, z: 4, core: 2. Of those that a mesh axis runs over, the one named last changes fastest.
Arguments:
- pixels: bfloat16 [8, 2, 13, 384, 192], P(('groups', 'date'), None, None, 'row', 'col'), parts along dimension 0, may hold values from -6 to 6
- w_stem: bfloat16 [64, 13, 7, 7], replicated, may hold values from -0.25 to 0.25
- w_head: float32 [64, 128], replicated, may hold values from -0.75 to 0.75
- pool_grid: int32 [192, 96], P('row', 'col'), may hold values from 0 to 71, as said below
- neg_index: int32 [8, 2, 24, 12, 128], P(('groups', 'date'), None, 'row', 'col'), parts along dimension 0, may hold values from 0 to 143
- key_date: int32 [4], replicated, may hold values from 0 to 3, as said below
Outputs:
- anchor_loss: float32 [8, 2, 24, 12], P(('groups', 'date'), None, 'row', 'col'), parts along dimension 0
- grad_stem: float32 [128, 13, 7, 7], P('groups'), parts along dimension 0
- grad_head: float32 [128, 128], P('groups'), parts along dimension 0
The draws below stay inside these ranges and needn't reach their ends.
There are 2 independent parts, one for each index of `groups`. The reference program is written for one: setup_inputs(seed, part) draws one part's arguments, and reference() takes and returns one part's arrays. A program takes and returns all parts, laid end to end along the dimension named above; an argument that names none is the same for every part. Nothing has to cross between parts.
Inputs may be any that keep to these rules, and one draw needn't show every extreme that they name: `pool_grid`: cell numbers are local to a device block of 96 x 48 stem outputs; every block names each of its 72 cells at least once. `neg_index`: entry k names key k = t * 72 + c of the same block: cell c of tile t on the paired date. Following d to key_date[d] runs once through all 4 dates and back; no date is its own key date.
All inputs are finite; a program needn't handle non-finite values.
Results may differ from the reference program's by a relative error of at most 0.0052.
Values may be sent and summed in bfloat16 or wider, within the bound.
A program may use at most 128 MiB of HBM per device.

```python
import math
import jax
import jax.numpy as jnp
from jax import lax

BANDS = 13
CH = 64
EMB = 128
TILES = 2
CELL = 8
NEG = 128
DATES = 4
FH = 96
FW = 48
CELLS_DEV = 72
KEYS = 144
CELLS_R = 24
CELLS_C = 12
FEAT_H = 192
FEAT_W = 96
TILE_H = 384
TILE_W = 192
N_ROW = 2
N_COL = 2


def draw_pool_grid(key, part):
    row_ids = jnp.arange(FEAT_H, dtype=jnp.int32)[:, None] % FH
    col_ids = jnp.arange(FEAT_W, dtype=jnp.int32)[None, :] % FW
    regular = row_ids // CELL * (FW // CELL) + col_ids // CELL
    corner = jnp.logical_and(row_ids % CELL == 0, col_ids % CELL == 0)
    first_key, second_key = jax.random.split(jax.random.fold_in(key, 17))
    moving = jax.random.randint(first_key, (FEAT_H, FEAT_W), 0, 4) == 0
    other = jax.random.randint(second_key, (FEAT_H, FEAT_W), 0, CELLS_DEV)
    chosen = jnp.where(jnp.logical_and(moving, jnp.logical_not(corner)), other, regular)
    return chosen.astype(jnp.int32)


def draw_key_date(key, part):
    first_key, second_key = jax.random.split(jax.random.fold_in(key, 29))
    values = jnp.arange(DATES, dtype=jnp.int32)
    fixed = jnp.array([0, DATES - 1, DATES // 2 - 1, DATES // 2], dtype=jnp.int32)
    order = jax.random.permutation(first_key, values)
    place = jnp.zeros((DATES,), jnp.int32).at[order].set(values)
    fixed_hit = values[:, None] == fixed[None, :]
    fixed_rank = jnp.sum(jnp.where(fixed_hit, jnp.arange(4, dtype=jnp.int32)[None, :], 0), axis=1)
    score = jnp.where(jnp.any(fixed_hit, axis=1), fixed_rank, 4 + place)
    sequence = jnp.argsort(score, stable=True).astype(jnp.int32)
    start = jax.random.randint(second_key, (), 0, DATES)
    sequence = (sequence + start) % DATES
    following = jnp.roll(sequence, -1)
    return jnp.zeros((DATES,), jnp.int32).at[sequence].set(following)


def with_ends(values, own_key, low, top_value):
    longest = values.shape.index(max(values.shape))
    spots = []
    for shift in (0, 1):
        where = [jax.random.randint(jax.random.fold_in(own_key, axis), (), 0, length) for axis, length in enumerate(values.shape)]
        where[longest] = (where[longest] + shift) % values.shape[longest]
        spots.append(tuple(where))
    return values.at[spots[0]].set(low).at[spots[1]].set(top_value)


def shard_levels(own_key, extent, shards, low, largest):
    def one(axis_at, shards_of):
        heights = jax.random.uniform(jax.random.fold_in(jax.random.fold_in(own_key, 6), axis_at), (shards_of,), jnp.float32, low / len(shards), largest / len(shards))
        return jnp.repeat(jnp.exp(heights), extent[axis_at] // shards_of).reshape((-1,) + (1,) * (len(extent) - axis_at - 1))

    loudness = one(*shards[0])
    for cut in shards[1:]:
        loudness = loudness * one(*cut)
    return loudness


def gaussian(own_key, shape, deviation, limit, cuts=(), kind=jnp.bfloat16):
    entries = jax.random.normal(own_key, shape, jnp.float32) * deviation
    if len(cuts) > 0:
        entries = shard_levels(own_key, shape, cuts, -0.22, 0.18) * entries
    return jnp.clip(entries, min=-limit, max=limit).astype(kind)


def setup_inputs(seed: int = 0, part: int = 0) -> dict:
    arg_keys = jax.random.split(jax.random.key(seed), 7)
    own_keys = jax.random.split(jax.random.fold_in(arg_keys[6], part), 7)
    return {
        "pixels": gaussian(own_keys[0], (DATES, TILES, BANDS, TILE_H, TILE_W), 1.0, 6.0, ((0, 4), (3, 2), (4, 2))),
        "w_stem": gaussian(arg_keys[1], (CH, BANDS, 7, 7), (BANDS * 49) ** -0.5, 0.25),
        "w_head": gaussian(arg_keys[2], (CH, EMB), CH ** -0.5, 0.75, (), jnp.float32),
        "pool_grid": draw_pool_grid(jax.random.fold_in(arg_keys[6], 71), part),
        "neg_index": with_ends(jax.random.randint(own_keys[4], (DATES, TILES, CELLS_R, CELLS_C, NEG), 0, KEYS), jax.random.fold_in(own_keys[4], 1), 0, KEYS - 1).astype(jnp.int32),
        "key_date": draw_key_date(jax.random.fold_in(arg_keys[6], 71), part),
    }


TEMP = 0.2
EPS = 1e-06

def stem_conv(padded, w_stem):
    return lax.conv_general_dilated(padded, w_stem, (2, 2), 'VALID', dimension_numbers=('NCHW', 'OIHW', 'NCHW'), preferred_element_type=jnp.float32)

def weight_term(padded, slope_low):
    left_side = jnp.transpose(padded, (1, 0, 2, 3))
    right_side = jnp.transpose(slope_low, (1, 0, 2, 3))
    result = lax.conv_general_dilated(left_side, right_side, (1, 1), 'VALID', rhs_dilation=(2, 2), dimension_numbers=('NCHW', 'OIHW', 'NCHW'), preferred_element_type=jnp.float32)
    return jnp.transpose(result, (1, 0, 2, 3))

def to_blocks(feature):
    shaped = feature.reshape(TILES, CH, N_ROW, FH, N_COL, FW)
    return shaped.transpose(2, 4, 0, 1, 3, 5).reshape(N_ROW, N_COL, TILES, CH, FH * FW)

def from_blocks(blocked):
    shaped = blocked.reshape(N_ROW, N_COL, TILES, CH, FH, FW)
    return shaped.transpose(2, 3, 0, 4, 1, 5).reshape(TILES, CH, FEAT_H, FEAT_W)

def reference(pixels, w_stem, w_head, pool_grid, neg_index, key_date):
    anchors = KEYS
    grid_blocks = pool_grid.reshape(N_ROW, FH, N_COL, FW).transpose(0, 2, 1, 3).reshape(N_ROW, N_COL, FH * FW)
    member = (grid_blocks[..., None] == jnp.arange(CELLS_DEV, dtype=jnp.int32)).astype(jnp.float32)
    counts = lax.optimization_barrier(jnp.sum(member, axis=2))

    def pad_tile(tile_data):
        return jnp.pad(tile_data, ((0, 0), (0, 0), (3, 2), (3, 2)))

    def forward_date(tile_data):
        stem_out = stem_conv(pad_tile(tile_data), w_stem)
        hidden = lax.optimization_barrier(jnp.maximum(stem_out, 0.0).astype(jnp.bfloat16)).astype(jnp.float32)
        cell_sums = jnp.einsum('rstcp,rspk->rstkc', to_blocks(hidden), member, precision=lax.Precision.HIGHEST)
        return cell_sums / counts[:, :, None, :, None]
    pooled = lax.map(forward_date, pixels).reshape(DATES, N_ROW, N_COL, anchors, CH)
    project = jnp.einsum('drsac,ce->drsae', pooled, w_head, precision=lax.Precision.HIGHEST)
    length = jnp.sqrt(lax.optimization_barrier(jnp.sum(project * project, axis=-1, keepdims=True)) + EPS)
    embed = project / length
    date_ids = jnp.arange(DATES, dtype=jnp.int32)
    source_date = jnp.zeros((DATES,), jnp.int32).at[key_date].set(date_ids)
    key_rows = embed[key_date]
    scores = jnp.einsum('drsae,drsbe->drsab', embed, key_rows, precision=lax.Precision.HIGHEST) / TEMP
    neg_rows = neg_index.reshape(DATES, TILES, N_ROW, FH // CELL, N_COL, FW // CELL, NEG)
    neg_rows = neg_rows.transpose(0, 2, 4, 1, 3, 5, 6).reshape(DATES, N_ROW, N_COL, anchors, NEG)
    negative = jnp.take_along_axis(scores, neg_rows, axis=-1)
    positive = jnp.diagonal(scores, axis1=-2, axis2=-1)
    denominator = jnp.exp(positive) + lax.optimization_barrier(jnp.sum(jnp.exp(negative), axis=-1))
    losses = jnp.log(denominator) - positive
    anchor_loss = losses.reshape(DATES, N_ROW, N_COL, TILES, FH // CELL, FW // CELL)
    anchor_loss = anchor_loss.transpose(0, 3, 1, 4, 2, 5).reshape(DATES, TILES, CELLS_R, CELLS_C)
    scale = 1.0 / math.sqrt(DATES * TILES * CELLS_R * CELLS_C)
    d_pos = scale * (jnp.exp(positive) / denominator - 1.0)
    d_neg = scale * jnp.exp(negative) / denominator[..., None]
    arange_rows = jnp.arange(anchors, dtype=jnp.int32)

    def scatter_one(rows_one, neg_one, pos_one):
        grid_zero = jnp.zeros((anchors, anchors), jnp.float32)
        grid_zero = grid_zero.at[arange_rows[:, None], rows_one].add(neg_one)
        return grid_zero.at[arange_rows, arange_rows].add(pos_one)
    d_scores = jax.vmap(scatter_one)(neg_rows.reshape(-1, anchors, NEG), d_neg.reshape(-1, anchors, NEG), d_pos.reshape(-1, anchors))
    d_scores = d_scores.reshape(DATES, N_ROW, N_COL, anchors, anchors) / TEMP
    grad_anchor = jnp.einsum('drsab,drsbe->drsae', d_scores, key_rows, precision=lax.Precision.HIGHEST)
    grad_keys = jnp.einsum('drsab,drsae->drsbe', d_scores, embed, precision=lax.Precision.HIGHEST)
    grad_embed = grad_anchor + grad_keys[source_date]
    grad_project = (grad_embed - embed * lax.optimization_barrier(jnp.sum(embed * grad_embed, axis=-1, keepdims=True))) / length
    grad_head = jnp.einsum('drsac,drsae->ce', pooled, grad_project, precision=lax.Precision.HIGHEST)
    grad_pooled = jnp.einsum('drsae,ce->drsac', grad_project, w_head, precision=lax.Precision.HIGHEST)
    per_cell = grad_pooled.reshape(DATES, N_ROW, N_COL, TILES, CELLS_DEV, CH) / counts[None, :, :, None, :, None]

    def backward_date(carry, inputs):
        tile_data, cell_grad = inputs
        padded = pad_tile(tile_data)
        stem_out = stem_conv(padded, w_stem)
        spread = jnp.einsum('rstkc,rspk->rstcp', cell_grad, member, precision=lax.Precision.HIGHEST)
        slope_low = jnp.where(stem_out > 0, from_blocks(spread), 0.0).astype(jnp.bfloat16)
        return (carry + weight_term(padded, slope_low), None)
    grad_stem, _ = lax.scan(backward_date, jnp.zeros((CH, BANDS, 7, 7), jnp.float32), (pixels, per_cell))
    return (anchor_loss, grad_stem, grad_head)
```

```python
import functools
import math

import jax
import jax.numpy as jnp
import numpy as np
from jax import lax
from jax.experimental import pallas as pl
from jax.experimental.pallas import tpu as pltpu
from jax.sharding import PartitionSpec as P

CELL = 8
TEMP = 0.2
EPS = 1e-06
STEP = 4
LANES = 128
HALF = 64

MESH = pl.DeviceIdType.MESH
HIGH = lax.Precision.HIGHEST
BF = jnp.bfloat16
F32 = jnp.float32


def mm(left, right):
    return lax.dot_general(left, right, (((1,), (0,)), ((), ())), preferred_element_type=F32)


def mm_nt(left, right, precision=None):
    return lax.dot_general(
        left, right, (((1,), (1,)), ((), ())), precision=precision, preferred_element_type=F32
    )


def mm_tn(left, right, precision=None):
    return lax.dot_general(
        left, right, (((0,), (0,)), ((), ())), precision=precision, preferred_element_type=F32
    )


def tables(tiles, bands, height, width):
    cols = np.zeros((tiles, width, 2 * LANES), np.float32)
    for t in range(tiles):
        for w in range(width):
            q = w + 3
            cols[t, w, (q % 2) * LANES + t * HALF + q // 2] = 1
    edge = np.zeros((tiles, 32, width), np.float32)
    halo = np.zeros((2, 16, 2 * LANES), np.float32)
    for t in range(tiles):
        for k in range(3):
            edge[t, t * 8 + k, width - 3 + k] = 1
            edge[t, 16 + t * 8 + k, k] = 1
            halo[0, t * 8 + k, (k % 2) * LANES + t * HALF + k // 2] = 1
            q = width + 3 + k
            halo[1, t * 8 + k, (q % 2) * LANES + t * HALF + q // 2] = 1
    rows = np.zeros((16, 16, 2, bands, 16), np.float32)
    for r in range(16):
        for c in range(bands):
            if r < 3:
                rows[r, c, 0, c, 13 + r] = 1
            else:
                rows[r, c, 1, c, r - 3] = 1
    rows = rows.reshape(256, 2 * bands * 16)
    taps = np.zeros((4, bands, 7, 8, 8, 2, 16), np.float32)
    for b in range(4):
        for c in range(bands):
            for u in range(7):
                for pc in range(2):
                    if 2 * b + pc < 7:
                        taps[b, c, u, 2 * b + pc, u, pc, c] = 1
    taps = taps.reshape(4, bands * 56, 256)
    return [jnp.asarray(x, BF) for x in (cols, edge, halo, rows, taps)]


def kernel(
    sizes,
    pix, w_taps, w_head, grid_t, neg, key_date, cols, edge, halo, rows, taps, place,
    loss_out, stem_out, head_out,
    pack, strips, blocks, image, w_all, gids, neg_t, count_t, member, hidden,
    keys, grads, g_acc, part, gather1, gather2, gather3,
    s_col, r_col, s_row, r_row, s_key, r_key, s_gra, r_gra, s_1, r_1, s_2, r_2, s_3, r_3,
):
    tiles, bands, height, width, n_row, n_col, dates = sizes
    fr, fc = height // 2, width // 2
    cells = fr // CELL * (fc // CELL)
    anchors = tiles * cells
    n_mem = n_row * n_col
    row, col, date = lax.axis_index("row"), lax.axis_index("col"), lax.axis_index("date")
    me = row * n_col + col

    barrier = pltpu.get_barrier_semaphore()
    members, peers = [], []
    for k in range(1, n_mem):
        other = lax.rem(me + k, n_mem)
        members.append((other, {"row": other // n_col, "col": lax.rem(other, n_col)}))
    for k in range(1, dates):
        other = lax.rem(date + k, dates)
        peers.append((other, {"date": other}))
    for _, dev in members + peers:
        pl.semaphore_signal(barrier, inc=1, device_id=dev, device_id_type=MESH)

    def pack_band(c, carry):
        both = mm_nt(edge[0], pix[0, c])
        for t in range(1, tiles):
            both += mm_nt(edge[t], pix[t, c])
        both = both.astype(BF)
        pack[0, c] = both[:16]
        pack[1, c] = both[16:]
        return carry

    lax.fori_loop(0, bands, pack_band, 0)
    pl.semaphore_wait(barrier, len(members) + len(peers))

    def copy(src, dst, send, recv, dev):
        return pltpu.make_async_remote_copy(
            src_ref=src, dst_ref=dst, send_sem=send, recv_sem=recv,
            device_id=dev, device_id_type=MESH,
        )

    to_right = copy(pack.at[0], strips.at[0], s_col.at[0], r_col.at[0], {"col": lax.rem(col + 1, n_col)})
    to_left = copy(pack.at[1], strips.at[1], s_col.at[1], r_col.at[1], {"col": lax.rem(col + n_col - 1, n_col)})
    down = copy(blocks.at[height // 16], blocks.at[0], s_row.at[0], r_row.at[0], {"row": lax.rem(row + 1, n_row)})
    up = copy(blocks.at[1], blocks.at[height // 16 + 1], s_row.at[1], r_row.at[1], {"row": lax.rem(row + n_row - 1, n_row)})

    @pl.when(col < n_col - 1)
    def _():
        to_right.start()

    @pl.when(col > 0)
    def _():
        to_left.start()

    @pl.when(col == 0)
    def _():
        strips[0] = jnp.zeros(strips.shape[1:], BF)

    @pl.when(col == n_col - 1)
    def _():
        strips[1] = jnp.zeros(strips.shape[1:], BF)

    for b in range(4):
        w_all[64 * b : 64 * b + 64, :] = mm_tn(w_taps[...], taps[b]).astype(BF)
    lane = lax.broadcasted_iota(jnp.int32, (1, LANES), 1)
    inside = lax.rem(lane, HALF) < fc
    shift = jnp.where(inside, (lane // HALF) * cells, -1000).astype(F32)
    gids[...] = mm_tn(grid_t[...].astype(F32).astype(BF), place[...]) + shift
    sub = lax.broadcasted_iota(jnp.int32, (anchors, 1), 0)
    key_ids = (lax.rem(sub, tiles) * cells + sub // tiles).astype(F32)
    eye_n = (
        lax.broadcasted_iota(jnp.int32, (neg.shape[1],) * 2, 0)
        == lax.broadcasted_iota(jnp.int32, (neg.shape[1],) * 2, 1)
    ).astype(F32).astype(BF)
    neg_t[...] = mm_nt(eye_n, neg[...].astype(F32).astype(BF))

    def count_step(s, total):
        for k in range(8):
            total += jnp.where(neg_t[pl.ds(s * 8 + k, 1), :] == key_ids, 1.0, 0.0)
        return total

    count_t[...] = lax.fori_loop(
        0, neg.shape[1] // 8, count_step, jnp.zeros((anchors, anchors), F32)
    )

    @pl.when(col > 0)
    def _():
        copy(pack.at[0], strips.at[0], s_col.at[0], r_col.at[0], {"col": lax.rem(col + n_col - 1, n_col)}).wait_recv()

    @pl.when(col < n_col - 1)
    def _():
        copy(pack.at[1], strips.at[1], s_col.at[1], r_col.at[1], {"col": lax.rem(col + 1, n_col)}).wait_recv()

    def own_band(c, carry):
        wide = mm_tn(strips[0, c], halo[0]) + mm_tn(strips[1, c], halo[1])
        for t in range(tiles):
            wide += mm(pix[t, c], cols[t])
        blocks[pl.ds(1, height // 16), c] = wide.astype(BF).reshape(height // 16, 16, 2 * LANES)
        return carry

    lax.fori_loop(0, bands, own_band, 0)

    @pl.when(row < n_row - 1)
    def _():
        down.start()

    @pl.when(row > 0)
    def _():
        up.start()

    @pl.when(row == 0)
    def _():
        blocks[0] = jnp.zeros(blocks.shape[1:], BF)

    @pl.when(row == n_row - 1)
    def _():
        blocks[height // 16 + 1] = jnp.zeros(blocks.shape[1:], BF)

    @pl.when(row > 0)
    def _():
        copy(blocks.at[height // 16], blocks.at[0], s_row.at[0], r_row.at[0], {"row": lax.rem(row + n_row - 1, n_row)}).wait_recv()

    @pl.when(row < n_row - 1)
    def _():
        copy(blocks.at[1], blocks.at[height // 16 + 1], s_row.at[1], r_row.at[1], {"row": lax.rem(row + 1, n_row)}).wait_recv()

    def image_step(k, carry):
        pair = blocks[pl.ds(k, 2)].reshape(2 * bands * 16, 2 * LANES)
        out = mm(rows[...], pair).astype(BF)
        for pc in range(2):
            image[pl.ds(k * 8, 8), :, pc] = out[:, pc * LANES : (pc + 1) * LANES].reshape(8, 2, 16, LANES)
        return carry

    lax.fori_loop(0, height // 16 + 1, image_step, 0)

    def wide_rows(s):
        return jnp.concatenate(
            [image[pl.ds(s * STEP + r, 4)].reshape(256, LANES) for r in range(STEP)], axis=1
        )

    def forward_step(s, total):
        taps_out = mm(w_all[...], wide_rows(s))
        hid, mem = [], []
        for r in range(STEP):
            part_r = taps_out[:, r * LANES : (r + 1) * LANES]
            stem = part_r[:64]
            for b in range(1, 4):
                stem += pltpu.roll(part_r[64 * b : 64 * b + 64], LANES - b, 1)
            hid.append(jnp.maximum(stem, 0.0).astype(BF))
            mem.append(jnp.where(gids[pl.ds(s * STEP + r, 1), :] == key_ids, 1.0, 0.0).astype(BF))
        hid = jnp.concatenate(hid, axis=1)
        mem = jnp.concatenate(mem, axis=1)
        hidden[s] = hid
        member[s] = mem
        return total + mm_nt(mem, jnp.concatenate([hid, jnp.ones_like(hid)], axis=0))

    sums = lax.fori_loop(0, fr // STEP, forward_step, jnp.zeros((anchors, LANES), F32))
    counts = sums[:, 64:]
    pooled = sums[:, :64] / counts
    head = w_head[...]
    project = lax.dot_general(
        pooled, head, (((1,), (0,)), ((), ())), precision=HIGH, preferred_element_type=F32
    )
    length = jnp.sqrt(jnp.sum(project * project, axis=1, keepdims=True) + EPS)
    embed = project / length
    keys[pl.ds(date, 1)] = embed[None]
    sends = [copy(keys.at[date], keys.at[date], s_key.at[o], r_key.at[date], dev) for o, dev in peers]
    for c in sends:
        c.start()
    for o, dev in peers:
        copy(keys.at[o], keys.at[o], s_key.at[o], r_key.at[o], dev).wait_recv()
    target = key_date[date]
    key_rows = keys[target]
    scores = mm_nt(key_rows, embed, HIGH) / TEMP
    same = lax.broadcasted_iota(jnp.int32, (anchors, anchors), 0) == lax.broadcasted_iota(
        jnp.int32, (anchors, anchors), 1
    )
    positive = jnp.sum(jnp.where(same, scores, 0.0), axis=0, keepdims=True)
    weights = count_t[...] * jnp.exp(scores)
    exp_pos = jnp.exp(positive)
    denominator = exp_pos + jnp.sum(weights, axis=0, keepdims=True)
    loss_out[...] = jnp.log(denominator) - positive
    scale = 1.0 / math.sqrt(dates * anchors * n_mem)
    d_scores = (scale / TEMP) * (
        weights / denominator + jnp.where(same, exp_pos / denominator - 1.0, 0.0)
    )
    grads[pl.ds(date, 1)] = lax.dot_general(
        d_scores, embed, (((1,), (0,)), ((), ())), precision=HIGH, preferred_element_type=F32
    )[None]
    more = [copy(grads.at[date], grads.at[date], s_gra.at[o], r_gra.at[date], dev) for o, dev in peers]
    for c in more:
        c.start()
    grad_anchor = mm_tn(d_scores, key_rows, HIGH)
    for o, dev in peers:
        copy(grads.at[o], grads.at[o], s_gra.at[o], r_gra.at[o], dev).wait_recv()
    returned = jnp.zeros_like(grad_anchor)
    for d in range(dates):
        returned += jnp.where(key_date[d] == date, grads[d], 0.0)
    grad_embed = grad_anchor + returned
    grad_project = (
        grad_embed - embed * jnp.sum(embed * grad_embed, axis=1, keepdims=True)
    ) / length
    head_term = mm_tn(pooled, grad_project, HIGH)
    per_cell = (mm_nt(grad_project, head, HIGH) / counts).astype(BF)
    eye_c = (
        lax.broadcasted_iota(jnp.int32, (64, 64), 0) == lax.broadcasted_iota(jnp.int32, (64, 64), 1)
    ).astype(F32).astype(BF)
    cell_t = mm_nt(eye_c, per_cell).astype(BF)

    g_acc[...] = jnp.zeros_like(g_acc)

    def backward_step(s, carry):
        spread = mm(cell_t, member[s])
        slope = jnp.where(hidden[s].astype(F32) > 0.0, spread, 0.0)
        moved = [slope.astype(BF)]
        for b in range(1, 4):
            moved.append(
                jnp.concatenate(
                    [pltpu.roll(slope[:, r * LANES : (r + 1) * LANES], b, 1) for r in range(STEP)],
                    axis=1,
                ).astype(BF)
            )
        g_acc[...] += mm_nt(jnp.concatenate(moved, axis=0), wide_rows(s))
        return carry

    lax.fori_loop(0, fr // STEP, backward_step, 0)

    gr, hr = 256 // n_mem, 64 // n_mem
    for m in range(n_mem):
        part[m, :gr] = g_acc[m * gr : (m + 1) * gr]
        part[m, gr:] = jnp.concatenate([head_term[m * hr : (m + 1) * hr]] * 2, axis=1)
    sends += more
    gather1[pl.ds(me, 1)] = part[pl.ds(me, 1)]
    step1 = [copy(part.at[o], gather1.at[me], s_1.at[o], r_1.at[me], dev) for o, dev in members]
    for c in step1:
        c.start()
    for o, dev in members:
        copy(part.at[o], gather1.at[o], s_1.at[o], r_1.at[o], dev).wait_recv()
    total = gather1[0]
    for m in range(1, n_mem):
        total += gather1[m]
    gather2[pl.ds(date, 1)] = total[None]
    step2 = [copy(gather2.at[date], gather2.at[date], s_2.at[o], r_2.at[date], dev) for o, dev in peers]
    for c in step2:
        c.start()
    for o, dev in peers:
        copy(gather2.at[o], gather2.at[o], s_2.at[o], r_2.at[o], dev).wait_recv()
    total = gather2[0]
    for d in range(1, dates):
        total += gather2[d]
    gather3[pl.ds(me, 1)] = total[None]
    step3 = [copy(gather3.at[me], gather3.at[me], s_3.at[o], r_3.at[me], dev) for o, dev in members]
    for c in step3:
        c.start()
    for o, dev in members:
        copy(gather3.at[o], gather3.at[o], s_3.at[o], r_3.at[o], dev).wait_recv()
    for m in range(n_mem):
        head_out[m * hr : (m + 1) * hr] = gather3[m, gr:, :LANES]
        g_acc[m * gr : (m + 1) * gr] = gather3[m, :gr]
    result = jnp.zeros((bands * 56, 64), F32)
    for b in range(4):
        whole = g_acc[64 * b : 64 * b + 64]
        high = whole.astype(BF)
        rest = whole - high.astype(F32)
        mid = rest.astype(BF)
        low = (rest - mid.astype(F32)).astype(BF)
        result += mm_nt(taps[b], high) + (mm_nt(taps[b], mid) + mm_nt(taps[b], low))
    stem_out[...] = result.reshape(bands, 7, 8, 64)[:, :, :7, :]

    for c in sends + step1 + step2 + step3:
        c.wait_send()

    @pl.when(col < n_col - 1)
    def _():
        to_right.wait_send()

    @pl.when(col > 0)
    def _():
        to_left.wait_send()

    @pl.when(row < n_row - 1)
    def _():
        down.wait_send()

    @pl.when(row > 0)
    def _():
        up.wait_send()


def solution(mesh):
    n_row, n_col, dates = mesh.shape["row"], mesh.shape["col"], mesh.shape["date"]

    def local(pixels, w_stem, w_head, pool_grid, neg_index, key_date):
        _, tiles, bands, height, width = pixels.shape
        fr, fc = height // 2, width // 2
        cells = fr // CELL * (fc // CELL)
        anchors = tiles * cells
        n_mem = n_row * n_col
        chunk = (256 + 64) // n_mem
        w_taps = jnp.pad(jnp.transpose(w_stem, (1, 2, 3, 0)), ((0, 0), (0, 0), (0, 1), (0, 0)))
        w_taps = w_taps.reshape(bands * 56, 64)
        grid_t = pool_grid.T
        neg = jnp.transpose(neg_index[0], (1, 2, 0, 3)).reshape(anchors, -1)
        place = np.zeros((fc, LANES), np.float32)
        for j in range(fc):
            for t in range(tiles):
                place[j, t * HALF + j] = 1
        vmem = pl.BlockSpec(memory_space=pltpu.VMEM)
        dma = pltpu.SemaphoreType.DMA
        loss, stem, head = pl.pallas_call(
            functools.partial(kernel, (tiles, bands, height, width, n_row, n_col, dates)),
            out_shape=(
                jax.ShapeDtypeStruct((1, anchors), F32),
                jax.ShapeDtypeStruct((bands, 7, 7, 64), F32),
                jax.ShapeDtypeStruct((64, LANES), F32),
            ),
            in_specs=[vmem] * 5 + [pl.BlockSpec(memory_space=pltpu.SMEM)] + [vmem] * 6,
            out_specs=(vmem, vmem, vmem),
            scratch_shapes=[
                pltpu.VMEM((2, bands, 16, height), BF),
                pltpu.VMEM((2, bands, 16, height), BF),
                pltpu.VMEM((height // 16 + 2, bands, 16, 2 * LANES), BF),
                pltpu.VMEM((height // 2 + 8, 2, 2, 16, LANES), BF),
                pltpu.VMEM((256, 256), BF),
                pltpu.VMEM((fr, LANES), F32),
                pltpu.VMEM((neg.shape[1], anchors), F32),
                pltpu.VMEM((anchors, anchors), F32),
                pltpu.VMEM((fr // STEP, anchors, STEP * LANES), BF),
                pltpu.VMEM((fr // STEP, 64, STEP * LANES), BF),
                pltpu.VMEM((dates, anchors, LANES), F32),
                pltpu.VMEM((dates, anchors, LANES), F32),
                pltpu.VMEM((256, 256), F32),
                pltpu.VMEM((n_mem, chunk, 256), F32),
                pltpu.VMEM((n_mem, chunk, 256), F32),
                pltpu.VMEM((dates, chunk, 256), F32),
                pltpu.VMEM((n_mem, chunk, 256), F32),
                dma((2,)), dma((2,)), dma((2,)), dma((2,)),
                dma((dates,)), dma((dates,)), dma((dates,)), dma((dates,)),
                dma((n_mem,)), dma((n_mem,)), dma((dates,)), dma((dates,)),
                dma((n_mem,)), dma((n_mem,)),
            ],
            compiler_params=pltpu.CompilerParams(
                collective_id=0, has_side_effects=True, vmem_limit_bytes=48 * 2**20
            ),
        )(
            pixels[0], w_taps, w_head, grid_t, neg, key_date,
            *tables(tiles, bands, height, width), jnp.asarray(place, BF),
        )
        loss = loss.reshape(fr // CELL, fc // CELL, tiles).transpose(2, 0, 1)[None]
        return loss, jnp.transpose(stem, (3, 0, 1, 2)), head

    return jax.shard_map(
        local,
        mesh=mesh,
        in_specs=(
            P(("groups", "date"), None, None, "row", "col"),
            P(),
            P(),
            P("row", "col"),
            P(("groups", "date"), None, "row", "col", None),
            P(),
        ),
        out_specs=(
            P(("groups", "date"), None, "row", "col"),
            P("groups", None, None, None),
            P("groups", None),
        ),
        check_vma=False,
    )
```

```python
import functools
import math

import jax
import jax.numpy as jnp
import numpy as np
from jax import lax
from jax.experimental import pallas as pl
from jax.experimental.pallas import tpu as pltpu
from jax.sharding import PartitionSpec as P

CELL = 8
TEMP = 0.2
EPS = 1e-06
STEP = 4
LANES = 128
HALF = 64

MESH = pl.DeviceIdType.MESH
HIGH = lax.Precision.HIGHEST
BF = jnp.bfloat16
F32 = jnp.float32


def mm(left, right):
    return lax.dot_general(left, right, (((1,), (0,)), ((), ())), preferred_element_type=F32)


def mm_high(left, right):
    return lax.dot_general(
        left, right, (((1,), (0,)), ((), ())), precision=HIGH, preferred_element_type=F32
    )


def fold(array):
    half = array.shape[0] // 2
    return jnp.concatenate([array[:half], array[half:]], axis=1)


def unfold(array):
    half = array.shape[1] // 2
    return jnp.concatenate([array[:, :half], array[:, half:]], axis=0)


def mm_nt(left, right, precision=None):
    return lax.dot_general(
        left, right, (((1,), (1,)), ((), ())), precision=precision, preferred_element_type=F32
    )


def mm_tn(left, right, precision=None):
    return lax.dot_general(
        left, right, (((0,), (0,)), ((), ())), precision=precision, preferred_element_type=F32
    )


def tables(tiles, bands, height, width):
    cols = np.zeros((tiles, width, 2 * LANES), np.float32)
    for t in range(tiles):
        for w in range(width):
            q = w + 3
            cols[t, w, (q % 2) * LANES + t * HALF + q // 2] = 1
    edge = np.zeros((tiles, 32, width), np.float32)
    halo = np.zeros((2, 16, 2 * LANES), np.float32)
    for t in range(tiles):
        for k in range(3):
            edge[t, t * 8 + k, width - 3 + k] = 1
            edge[t, 16 + t * 8 + k, k] = 1
            halo[0, t * 8 + k, (k % 2) * LANES + t * HALF + k // 2] = 1
            q = width + 3 + k
            halo[1, t * 8 + k, (q % 2) * LANES + t * HALF + q // 2] = 1
    rows = np.zeros((16, 16, 2, bands, 16), np.float32)
    for r in range(16):
        for c in range(bands):
            if r < 3:
                rows[r, c, 0, c, 13 + r] = 1
            else:
                rows[r, c, 1, c, r - 3] = 1
    rows = rows.reshape(256, 2 * bands * 16)
    taps = np.zeros((4, bands, 7, 8, 8, 2, 16), np.float32)
    for b in range(4):
        for c in range(bands):
            for u in range(7):
                for pc in range(2):
                    if 2 * b + pc < 7:
                        taps[b, c, u, 2 * b + pc, u, pc, c] = 1
    taps = taps.reshape(4, bands * 56, 256)
    return [jnp.asarray(x, BF) for x in (cols, edge, halo, rows, taps)]


def kernel(
    sizes,
    *refs,
):
    n_in = 12
    sources, (loss_out, stem_out, head_out) = refs[:n_in], refs[n_in : n_in + 3]
    held, rest = refs[n_in + 3 : 2 * n_in + 3], refs[2 * n_in + 3 :]
    pix, edge, w_taps, taps, grid_t, place, neg, cols, halo, rows, w_head, key_date = held
    body(sizes, sources, held, loss_out, stem_out, head_out,
         pix, edge, w_taps, taps, grid_t, place, neg, cols, halo, rows, w_head, key_date, *rest)


def body(
    sizes, sources, held, loss_out, stem_out, head_out,
    pix, edge, w_taps, taps, grid_t, place, neg, cols, halo, rows, w_head, key_date,
    pack, strips, blocks, image, w_all, gids, neg_t, count_t, member, hidden,
    keys, grads, g_acc, part, gather1, gather2, gather3,
    s_col, r_col, s_row, r_row, s_key, r_key, s_gra, r_gra, s_1, r_1, s_2, r_2, s_3, r_3, s_in,
):
    tiles, bands, height, width, n_row, n_col, dates = sizes
    fr, fc = height // 2, width // 2
    cells = fr // CELL * (fc // CELL)
    anchors = tiles * cells
    n_mem = n_row * n_col
    row, col, date = lax.axis_index("row"), lax.axis_index("col"), lax.axis_index("date")
    me = row * n_col + col

    fetches = [pltpu.make_async_copy(a, b, s_in.at[i]) for i, (a, b) in enumerate(zip(sources, held))]
    for c in fetches:
        c.start()
    barrier = pltpu.get_barrier_semaphore()
    members, peers = [], []
    for k in range(1, n_mem):
        other = lax.rem(me + k, n_mem)
        members.append((other, {"row": other // n_col, "col": lax.rem(other, n_col)}))
    for k in range(1, dates):
        other = lax.rem(date + k, dates)
        peers.append((other, {"date": other}))
    for _, dev in members + peers:
        pl.semaphore_signal(barrier, inc=1, device_id=dev, device_id_type=MESH)

    fetches[0].wait()
    fetches[1].wait()

    def pack_band(c, carry):
        both = mm_nt(edge[0], pix[0, c])
        for t in range(1, tiles):
            both += mm_nt(edge[t], pix[t, c])
        both = both.astype(BF)
        pack[0, c] = both[:16]
        pack[1, c] = both[16:]
        return carry

    lax.fori_loop(0, bands, pack_band, 0, unroll=True)
    pl.semaphore_wait(barrier, len(members) + len(peers))

    def copy(src, dst, send, recv, dev):
        return pltpu.make_async_remote_copy(
            src_ref=src, dst_ref=dst, send_sem=send, recv_sem=recv,
            device_id=dev, device_id_type=MESH,
        )

    to_right = copy(pack.at[0], strips.at[0], s_col.at[0], r_col.at[0], {"col": lax.rem(col + 1, n_col)})
    to_left = copy(pack.at[1], strips.at[1], s_col.at[1], r_col.at[1], {"col": lax.rem(col + n_col - 1, n_col)})
    down = copy(blocks.at[height // 16], blocks.at[0], s_row.at[0], r_row.at[0], {"row": lax.rem(row + 1, n_row)})
    up = copy(blocks.at[1], blocks.at[height // 16 + 1], s_row.at[1], r_row.at[1], {"row": lax.rem(row + n_row - 1, n_row)})

    @pl.when(col < n_col - 1)
    def _():
        to_right.start()

    @pl.when(col > 0)
    def _():
        to_left.start()

    @pl.when(col == 0)
    def _():
        strips[0] = jnp.zeros(strips.shape[1:], BF)

    @pl.when(col == n_col - 1)
    def _():
        strips[1] = jnp.zeros(strips.shape[1:], BF)

    for c in fetches[2:]:
        c.wait()
    for b in range(4):
        w_all[64 * b : 64 * b + 64, :] = mm_tn(w_taps[...], taps[b]).astype(BF)
    lane = lax.broadcasted_iota(jnp.int32, (1, LANES), 1)
    inside = lax.rem(lane, HALF) < fc
    shift = jnp.where(inside, (lane // HALF) * cells, -1000).astype(F32)
    gids[...] = mm_tn(grid_t[...].astype(F32).astype(BF), place[...]) + shift
    sub = lax.broadcasted_iota(jnp.int32, (anchors, 1), 0)
    key_ids = (lax.rem(sub, tiles) * cells + sub // tiles).astype(F32)
    eye_n = (
        lax.broadcasted_iota(jnp.int32, (neg.shape[1],) * 2, 0)
        == lax.broadcasted_iota(jnp.int32, (neg.shape[1],) * 2, 1)
    ).astype(F32).astype(BF)
    neg_t[...] = mm_nt(eye_n, neg[...].astype(F32).astype(BF))

    def count_step(s, total):
        for k in range(8):
            total += jnp.where(neg_t[pl.ds(s * 8 + k, 1), :] == key_ids, 1.0, 0.0)
        return total

    count_t[...] = lax.fori_loop(
        0, neg.shape[1] // 8, count_step, jnp.zeros((anchors, anchors), F32)
    )

    @pl.when(col > 0)
    def _():
        copy(pack.at[0], strips.at[0], s_col.at[0], r_col.at[0], {"col": lax.rem(col + n_col - 1, n_col)}).wait_recv()

    @pl.when(col < n_col - 1)
    def _():
        copy(pack.at[1], strips.at[1], s_col.at[1], r_col.at[1], {"col": lax.rem(col + 1, n_col)}).wait_recv()

    def own_band(c, carry):
        wide = mm_tn(strips[0, c], halo[0]) + mm_tn(strips[1, c], halo[1])
        for t in range(tiles):
            wide += mm(pix[t, c], cols[t])
        blocks[pl.ds(1, height // 16), c] = wide.astype(BF).reshape(height // 16, 16, 2 * LANES)
        return carry

    lax.fori_loop(0, bands, own_band, 0, unroll=True)

    @pl.when(row < n_row - 1)
    def _():
        down.start()

    @pl.when(row > 0)
    def _():
        up.start()

    @pl.when(row == 0)
    def _():
        blocks[0] = jnp.zeros(blocks.shape[1:], BF)

    @pl.when(row == n_row - 1)
    def _():
        blocks[height // 16 + 1] = jnp.zeros(blocks.shape[1:], BF)

    @pl.when(row > 0)
    def _():
        copy(blocks.at[height // 16], blocks.at[0], s_row.at[0], r_row.at[0], {"row": lax.rem(row + n_row - 1, n_row)}).wait_recv()

    @pl.when(row < n_row - 1)
    def _():
        copy(blocks.at[1], blocks.at[height // 16 + 1], s_row.at[1], r_row.at[1], {"row": lax.rem(row + 1, n_row)}).wait_recv()

    def image_step(k, carry):
        pair = blocks[pl.ds(k, 2)].reshape(2 * bands * 16, 2 * LANES)
        out = mm(rows[...], pair).astype(BF)
        for pc in range(2):
            image[pl.ds(k * 8, 8), :, pc] = out[:, pc * LANES : (pc + 1) * LANES].reshape(8, 2, 16, LANES)
        return carry

    lax.fori_loop(0, height // 16 + 1, image_step, 0, unroll=True)

    def wide_rows(s):
        return jnp.concatenate(
            [image[pl.ds(s * STEP + r, 4)].reshape(256, LANES) for r in range(STEP)], axis=1
        )

    def forward_step(s, total):
        taps_out = mm(w_all[...], wide_rows(s))
        hid, mem = [], []
        for r in range(STEP):
            part_r = taps_out[:, r * LANES : (r + 1) * LANES]
            stem = part_r[:64]
            for b in range(1, 4):
                stem += pltpu.roll(part_r[64 * b : 64 * b + 64], LANES - b, 1)
            hid.append(jnp.maximum(stem, 0.0).astype(BF))
            mem.append(jnp.where(gids[pl.ds(s * STEP + r, 1), :] == key_ids, 1.0, 0.0).astype(BF))
        hid = jnp.concatenate(hid, axis=1)
        mem = jnp.concatenate(mem, axis=1)
        hidden[s] = hid
        member[s] = mem
        return total + mm_nt(mem, jnp.concatenate([hid, jnp.ones_like(hid)], axis=0))

    sums = lax.fori_loop(0, fr // STEP, forward_step, jnp.zeros((anchors, LANES), F32))
    counts = sums[:, 64:]
    pooled = sums[:, :64] / counts
    head = w_head[...]
    project = mm_high(pooled, head)
    length = jnp.sqrt(jnp.sum(project * project, axis=1, keepdims=True) + EPS)
    embed = project / length
    short = pooled / length
    keys[pl.ds(date, 1)] = fold(short)[None]
    sends = [copy(keys.at[date], keys.at[date], s_key.at[o], r_key.at[date], dev) for o, dev in peers]
    for c in sends:
        c.start()
    back = mm_nt(embed, head, HIGH)
    for o, dev in peers:
        copy(keys.at[o], keys.at[o], s_key.at[o], r_key.at[o], dev).wait_recv()
    target = key_date[date]
    key_short = unfold(keys[target])
    scores = mm_nt(key_short, back, HIGH) / TEMP
    same = lax.broadcasted_iota(jnp.int32, (anchors, anchors), 0) == lax.broadcasted_iota(
        jnp.int32, (anchors, anchors), 1
    )
    positive = jnp.sum(jnp.where(same, scores, 0.0), axis=0, keepdims=True)
    weights = count_t[...] * jnp.exp(scores)
    exp_pos = jnp.exp(positive)
    denominator = exp_pos + jnp.sum(weights, axis=0, keepdims=True)
    scale = 1.0 / math.sqrt(dates * anchors * n_mem)
    d_scores = (scale / TEMP) * (
        weights / denominator + jnp.where(same, exp_pos / denominator - 1.0, 0.0)
    )
    grads[pl.ds(date, 1)] = fold(mm_high(d_scores, short))[None]
    more = [copy(grads.at[date], grads.at[date], s_gra.at[o], r_gra.at[date], dev) for o, dev in peers]
    for c in more:
        c.start()
    grad_short = mm_tn(d_scores, key_short, HIGH)
    losses = jnp.log(denominator) - positive
    n_down, n_across = fr // CELL, fc // CELL
    wide = n_across * tiles
    spot = lax.broadcasted_iota(jnp.int32, (wide, anchors), 1)
    pick = jnp.where(lax.rem(spot, wide) == lax.broadcasted_iota(jnp.int32, (wide, anchors), 0), losses, 0.0)
    line = lax.broadcasted_iota(jnp.int32, (n_down, anchors), 1) // wide
    lines = (line == lax.broadcasted_iota(jnp.int32, (n_down, anchors), 0)).astype(F32)
    loss_out[...] = mm_nt(pick, lines, HIGH).reshape(n_across, tiles, n_down)
    for o, dev in peers:
        copy(grads.at[o], grads.at[o], s_gra.at[o], r_gra.at[o], dev).wait_recv()
    returned = jnp.zeros(grads.shape[1:], F32)
    for d in range(dates):
        returned += jnp.where(key_date[d] == date, grads[d], 0.0)
    grad_embed = mm_high(grad_short + unfold(returned), head)
    grad_project = (
        grad_embed - embed * jnp.sum(embed * grad_embed, axis=1, keepdims=True)
    ) / length
    head_term = mm_tn(pooled, grad_project, HIGH)
    per_cell = (mm_nt(grad_project, head, HIGH) / counts).astype(BF)
    eye_c = (
        lax.broadcasted_iota(jnp.int32, (64, 64), 0) == lax.broadcasted_iota(jnp.int32, (64, 64), 1)
    ).astype(F32).astype(BF)
    cell_t = mm_nt(eye_c, per_cell).astype(BF)

    g_acc[...] = jnp.zeros_like(g_acc)

    def backward_step(s, carry):
        spread = mm(cell_t, member[s])
        slope = jnp.where(hidden[s].astype(F32) > 0.0, spread, 0.0)
        moved = [slope.astype(BF)]
        for b in range(1, 4):
            moved.append(
                jnp.concatenate(
                    [pltpu.roll(slope[:, r * LANES : (r + 1) * LANES], b, 1) for r in range(STEP)],
                    axis=1,
                ).astype(BF)
            )
        g_acc[...] += mm_nt(jnp.concatenate(moved, axis=0), wide_rows(s))
        return carry

    lax.fori_loop(0, fr // STEP, backward_step, 0)

    gr, hr = 256 // n_mem, 64 // n_mem
    for m in range(n_mem):
        part[m, :gr] = g_acc[m * gr : (m + 1) * gr].astype(BF)
        part[m, gr:] = jnp.concatenate([head_term[m * hr : (m + 1) * hr]] * 2, axis=1).astype(BF)
    sends += more
    gather1[pl.ds(me, 1)] = part[pl.ds(me, 1)]
    step1 = [copy(part.at[o], gather1.at[me], s_1.at[o], r_1.at[me], dev) for o, dev in members]
    for c in step1:
        c.start()
    for o, dev in members:
        copy(part.at[o], gather1.at[o], s_1.at[o], r_1.at[o], dev).wait_recv()
    total = gather1[0].astype(F32)
    for m in range(1, n_mem):
        total += gather1[m].astype(F32)
    gather2[pl.ds(date, 1)] = total.astype(BF)[None]
    step2 = [copy(gather2.at[date], gather2.at[date], s_2.at[o], r_2.at[date], dev) for o, dev in peers]
    for c in step2:
        c.start()
    for o, dev in peers:
        copy(gather2.at[o], gather2.at[o], s_2.at[o], r_2.at[o], dev).wait_recv()
    total = gather2[0].astype(F32)
    for d in range(1, dates):
        total += gather2[d].astype(F32)
    gather3[pl.ds(me, 1)] = total.astype(BF)[None]
    step3 = [copy(gather3.at[me], gather3.at[me], s_3.at[o], r_3.at[me], dev) for o, dev in members]
    for c in step3:
        c.start()
    for o, dev in members:
        copy(gather3.at[o], gather3.at[o], s_3.at[o], r_3.at[o], dev).wait_recv()
    for m in range(n_mem):
        head_out[m * hr : (m + 1) * hr] = gather3[m, gr:, :LANES].astype(F32)
    result = jnp.zeros((bands * 56, 64), F32)
    whole = jnp.concatenate([gather3[m, :gr] for m in range(n_mem)], axis=0)
    for b in range(4):
        result += mm_nt(taps[b], whole[64 * b : 64 * b + 64])
    stem_out[...] = result.reshape(bands, 7, 8, 64)[:, :, :7, :]

    for c in sends + step1 + step2 + step3:
        c.wait_send()

    @pl.when(col < n_col - 1)
    def _():
        to_right.wait_send()

    @pl.when(col > 0)
    def _():
        to_left.wait_send()

    @pl.when(row < n_row - 1)
    def _():
        down.wait_send()

    @pl.when(row > 0)
    def _():
        up.wait_send()


def solution(mesh):
    n_row, n_col, dates = mesh.shape["row"], mesh.shape["col"], mesh.shape["date"]

    def local(pixels, w_stem, w_head, pool_grid, neg_index, key_date):
        _, tiles, bands, height, width = pixels.shape
        fr, fc = height // 2, width // 2
        cells = fr // CELL * (fc // CELL)
        anchors = tiles * cells
        n_mem = n_row * n_col
        chunk = (256 + 64) // n_mem
        w_taps = jnp.pad(jnp.transpose(w_stem, (1, 2, 3, 0)), ((0, 0), (0, 0), (0, 1), (0, 0)))
        w_taps = w_taps.reshape(bands * 56, 64)
        grid_t = pool_grid.T
        neg = jnp.transpose(neg_index[0], (1, 2, 0, 3)).reshape(anchors, -1)
        place = np.zeros((fc, LANES), np.float32)
        for j in range(fc):
            for t in range(tiles):
                place[j, t * HALF + j] = 1
        vmem = pl.BlockSpec(memory_space=pltpu.VMEM)
        dma = pltpu.SemaphoreType.DMA
        cols, edge, halo, rows, taps = tables(tiles, bands, height, width)
        operands = (
            pixels[0], edge, w_taps, taps, grid_t, jnp.asarray(place, BF), neg, cols, halo, rows,
            w_head, key_date,
        )
        loss, stem, head = pl.pallas_call(
            functools.partial(kernel, (tiles, bands, height, width, n_row, n_col, dates)),
            out_shape=(
                jax.ShapeDtypeStruct((fc // CELL, tiles, fr // CELL), F32),
                jax.ShapeDtypeStruct((bands, 7, 7, 64), F32),
                jax.ShapeDtypeStruct((64, LANES), F32),
            ),
            in_specs=[pl.BlockSpec(memory_space=pltpu.HBM)] * len(operands),
            out_specs=(vmem, vmem, vmem),
            scratch_shapes=[pltpu.VMEM(x.shape, x.dtype) for x in operands[:-1]]
            + [pltpu.SMEM(key_date.shape, key_date.dtype)]
            + [
                pltpu.VMEM((2, bands, 16, height), BF),
                pltpu.VMEM((2, bands, 16, height), BF),
                pltpu.VMEM((height // 16 + 2, bands, 16, 2 * LANES), BF),
                pltpu.VMEM((height // 2 + 8, 2, 2, 16, LANES), BF),
                pltpu.VMEM((256, 256), BF),
                pltpu.VMEM((fr, LANES), F32),
                pltpu.VMEM((neg.shape[1], anchors), F32),
                pltpu.VMEM((anchors, anchors), F32),
                pltpu.VMEM((fr // STEP, anchors, STEP * LANES), BF),
                pltpu.VMEM((fr // STEP, 64, STEP * LANES), BF),
                pltpu.VMEM((dates, anchors // 2, LANES), F32),
                pltpu.VMEM((dates, anchors // 2, LANES), F32),
                pltpu.VMEM((256, 256), F32),
                pltpu.VMEM((n_mem, chunk, 256), BF),
                pltpu.VMEM((n_mem, chunk, 256), BF),
                pltpu.VMEM((dates, chunk, 256), BF),
                pltpu.VMEM((n_mem, chunk, 256), BF),
                dma((2,)), dma((2,)), dma((2,)), dma((2,)),
                dma((dates,)), dma((dates,)), dma((dates,)), dma((dates,)),
                dma((n_mem,)), dma((n_mem,)), dma((dates,)), dma((dates,)),
                dma((n_mem,)), dma((n_mem,)), dma((len(operands),)),
            ],
            compiler_params=pltpu.CompilerParams(
                collective_id=0, has_side_effects=True, vmem_limit_bytes=60 * 2**20
            ),
        )(*operands)
        loss = loss.transpose(1, 2, 0)[None]
        return loss, jnp.transpose(stem, (3, 0, 1, 2)), head

    return jax.shard_map(
        local,
        mesh=mesh,
        in_specs=(
            P(("groups", "date"), None, None, "row", "col"),
            P(),
            P(),
            P("row", "col"),
            P(("groups", "date"), None, "row", "col", None),
            P(),
        ),
        out_specs=(
            P(("groups", "date"), None, "row", "col"),
            P("groups", None, None, None),
            P("groups", None),
        ),
        check_vma=False,
    )
```

```python
import functools
import math

import jax
import jax.numpy as jnp
import numpy as np
from jax import lax
from jax.experimental import pallas as pl
from jax.experimental.pallas import tpu as pltpu
from jax.sharding import PartitionSpec as P

CELL = 8
TEMP = 0.2
EPS = 1e-06
STEP = 24
LANES = 128
HALF = 64

MESH = pl.DeviceIdType.MESH
HIGH = lax.Precision.HIGHEST
BF = jnp.bfloat16
F32 = jnp.float32


def mm(left, right):
    return lax.dot_general(left, right, (((1,), (0,)), ((), ())), preferred_element_type=F32)


def mm_high(left, right):
    return lax.dot_general(
        left, right, (((1,), (0,)), ((), ())), precision=HIGH, preferred_element_type=F32
    )


def fold(array):
    half = array.shape[0] // 2
    return jnp.concatenate([array[:half], array[half:]], axis=1)


def unfold(array):
    half = array.shape[1] // 2
    return jnp.concatenate([array[:, :half], array[:, half:]], axis=0)


def mm_nt(left, right, precision=None):
    return lax.dot_general(
        left, right, (((1,), (1,)), ((), ())), precision=precision, preferred_element_type=F32
    )


def mm_tn(left, right, precision=None):
    return lax.dot_general(
        left, right, (((0,), (0,)), ((), ())), precision=precision, preferred_element_type=F32
    )


def tables(tiles, bands, height, width):
    cols = np.zeros((tiles, width, 2 * LANES), np.float32)
    for t in range(tiles):
        for w in range(width):
            q = w + 3
            cols[t, w, (q % 2) * LANES + t * HALF + q // 2] = 1
    edge = np.zeros((tiles, 32, width), np.float32)
    halo = np.zeros((2, 16, 2 * LANES), np.float32)
    for t in range(tiles):
        for k in range(3):
            edge[t, t * 8 + k, width - 3 + k] = 1
            edge[t, 16 + t * 8 + k, k] = 1
            halo[0, t * 8 + k, (k % 2) * LANES + t * HALF + k // 2] = 1
            q = width + 3 + k
            halo[1, t * 8 + k, (q % 2) * LANES + t * HALF + q // 2] = 1
    rows = np.zeros((16, 16, 2, bands, 16), np.float32)
    for r in range(16):
        for c in range(bands):
            if r < 3:
                rows[r, c, 0, c, 13 + r] = 1
            else:
                rows[r, c, 1, c, r - 3] = 1
    rows = rows.reshape(256, 2 * bands * 16)
    taps = np.zeros((4, bands, 7, 8, 8, 2, 16), np.float32)
    for b in range(4):
        for c in range(bands):
            for u in range(7):
                for pc in range(2):
                    if 2 * b + pc < 7:
                        taps[b, c, u, 2 * b + pc, u, pc, c] = 1
    taps = taps.reshape(4, bands * 56, 256)
    return [jnp.asarray(x, BF) for x in (cols, edge, halo, rows, taps)]


def kernel(
    sizes,
    *refs,
):
    n_in = 12
    sources, (loss_out, stem_out, head_out) = refs[:n_in], refs[n_in : n_in + 3]
    held, rest = refs[n_in + 3 : 2 * n_in + 3], refs[2 * n_in + 3 :]
    pix, edge, w_taps, taps, grid_t, place, neg, cols, halo, rows, w_head, key_date = held
    body(sizes, sources, held, loss_out, stem_out, head_out,
         pix, edge, w_taps, taps, grid_t, place, neg, cols, halo, rows, w_head, key_date, *rest)


def body(
    sizes, sources, held, loss_out, stem_out, head_out,
    pix, edge, w_taps, taps, grid_t, place, neg, cols, halo, rows, w_head, key_date,
    pack, strips, blocks, image, w_all, gids, neg_t, count_t, member, hidden,
    keys, grads, g_acc, part, gather1, gather2, gather3,
    s_col, r_col, s_row, r_row, s_key, r_key, s_gra, r_gra, s_1, r_1, s_2, r_2, s_3, r_3, s_in,
):
    tiles, bands, height, width, n_row, n_col, dates = sizes
    fr, fc = height // 2, width // 2
    cells = fr // CELL * (fc // CELL)
    anchors = tiles * cells
    n_mem = n_row * n_col
    row, col, date = lax.axis_index("row"), lax.axis_index("col"), lax.axis_index("date")
    me = row * n_col + col

    fetches = [pltpu.make_async_copy(a, b, s_in.at[i]) for i, (a, b) in enumerate(zip(sources, held))]
    for c in fetches:
        c.start()
    barrier = pltpu.get_barrier_semaphore()
    members, peers = [], []
    for k in range(1, n_mem):
        other = lax.rem(me + k, n_mem)
        members.append((other, {"row": other // n_col, "col": lax.rem(other, n_col)}))
    for k in range(1, dates):
        other = lax.rem(date + k, dates)
        peers.append((other, {"date": other}))
    for _, dev in members + peers:
        pl.semaphore_signal(barrier, inc=1, device_id=dev, device_id_type=MESH)

    fetches[0].wait()
    fetches[1].wait()

    def pack_band(c, carry):
        both = mm_nt(edge[0], pix[0, c])
        for t in range(1, tiles):
            both += mm_nt(edge[t], pix[t, c])
        both = both.astype(BF)
        pack[0, c] = both[:16]
        pack[1, c] = both[16:]
        return carry

    lax.fori_loop(0, bands, pack_band, 0, unroll=True)
    pl.semaphore_wait(barrier, len(members) + len(peers))

    def copy(src, dst, send, recv, dev):
        return pltpu.make_async_remote_copy(
            src_ref=src, dst_ref=dst, send_sem=send, recv_sem=recv,
            device_id=dev, device_id_type=MESH,
        )

    to_right = copy(pack.at[0], strips.at[0], s_col.at[0], r_col.at[0], {"col": lax.rem(col + 1, n_col)})
    to_left = copy(pack.at[1], strips.at[1], s_col.at[1], r_col.at[1], {"col": lax.rem(col + n_col - 1, n_col)})
    down = copy(blocks.at[height // 16], blocks.at[0], s_row.at[0], r_row.at[0], {"row": lax.rem(row + 1, n_row)})
    up = copy(blocks.at[1], blocks.at[height // 16 + 1], s_row.at[1], r_row.at[1], {"row": lax.rem(row + n_row - 1, n_row)})

    @pl.when(col < n_col - 1)
    def _():
        to_right.start()

    @pl.when(col > 0)
    def _():
        to_left.start()

    @pl.when(col == 0)
    def _():
        strips[0] = jnp.zeros(strips.shape[1:], BF)

    @pl.when(col == n_col - 1)
    def _():
        strips[1] = jnp.zeros(strips.shape[1:], BF)

    for c in fetches[2:]:
        c.wait()
    for b in range(4):
        w_all[64 * b : 64 * b + 64, :] = mm_tn(w_taps[...], taps[b]).astype(BF)
    lane = lax.broadcasted_iota(jnp.int32, (1, LANES), 1)
    inside = lax.rem(lane, HALF) < fc
    shift = jnp.where(inside, (lane // HALF) * cells, -1000).astype(F32)
    gids[...] = mm_tn(grid_t[...].astype(F32).astype(BF), place[...]) + shift
    sub = lax.broadcasted_iota(jnp.int32, (anchors, 1), 0)
    key_ids = (lax.rem(sub, tiles) * cells + sub // tiles).astype(F32)
    eye_n = (
        lax.broadcasted_iota(jnp.int32, (neg.shape[1],) * 2, 0)
        == lax.broadcasted_iota(jnp.int32, (neg.shape[1],) * 2, 1)
    ).astype(F32).astype(BF)
    neg_t[...] = mm_nt(eye_n, neg[...].astype(F32).astype(BF))

    def count_step(s, total):
        for k in range(8):
            total += jnp.where(neg_t[pl.ds(s * 8 + k, 1), :] == key_ids, 1.0, 0.0)
        return total

    count_t[...] = lax.fori_loop(
        0, neg.shape[1] // 8, count_step, jnp.zeros((anchors, anchors), F32)
    )

    @pl.when(col > 0)
    def _():
        copy(pack.at[0], strips.at[0], s_col.at[0], r_col.at[0], {"col": lax.rem(col + n_col - 1, n_col)}).wait_recv()

    @pl.when(col < n_col - 1)
    def _():
        copy(pack.at[1], strips.at[1], s_col.at[1], r_col.at[1], {"col": lax.rem(col + 1, n_col)}).wait_recv()

    def own_band(c, carry):
        wide = mm_tn(strips[0, c], halo[0]) + mm_tn(strips[1, c], halo[1])
        for t in range(tiles):
            wide += mm(pix[t, c], cols[t])
        blocks[pl.ds(1, height // 16), c] = wide.astype(BF).reshape(height // 16, 16, 2 * LANES)
        return carry

    lax.fori_loop(0, bands, own_band, 0, unroll=True)

    @pl.when(row < n_row - 1)
    def _():
        down.start()

    @pl.when(row > 0)
    def _():
        up.start()

    @pl.when(row == 0)
    def _():
        blocks[0] = jnp.zeros(blocks.shape[1:], BF)

    @pl.when(row == n_row - 1)
    def _():
        blocks[height // 16 + 1] = jnp.zeros(blocks.shape[1:], BF)

    @pl.when(row > 0)
    def _():
        copy(blocks.at[height // 16], blocks.at[0], s_row.at[0], r_row.at[0], {"row": lax.rem(row + n_row - 1, n_row)}).wait_recv()

    @pl.when(row < n_row - 1)
    def _():
        copy(blocks.at[1], blocks.at[height // 16 + 1], s_row.at[1], r_row.at[1], {"row": lax.rem(row + 1, n_row)}).wait_recv()

    def image_step(k, carry):
        pair = blocks[pl.ds(k, 2)].reshape(2 * bands * 16, 2 * LANES)
        out = mm(rows[...], pair).astype(BF)
        for pc in range(2):
            image[pl.ds(k * 8, 8), :, pc] = out[:, pc * LANES : (pc + 1) * LANES].reshape(8, 2, 16, LANES)
        return carry

    lax.fori_loop(0, height // 16 + 1, image_step, 0, unroll=True)

    def wide_rows(s):
        return jnp.concatenate(
            [image[pl.ds(s * STEP + r, 4)].reshape(256, LANES) for r in range(STEP)], axis=1
        )

    def forward_step(s, total):
        taps_out = mm(w_all[...], wide_rows(s))
        hid, mem = [], []
        for r in range(STEP):
            part_r = taps_out[:, r * LANES : (r + 1) * LANES]
            stem = part_r[:64]
            for b in range(1, 4):
                stem += pltpu.roll(part_r[64 * b : 64 * b + 64], LANES - b, 1)
            hid.append(jnp.maximum(stem, 0.0).astype(BF))
            mem.append(jnp.where(gids[pl.ds(s * STEP + r, 1), :] == key_ids, 1.0, 0.0).astype(BF))
        hid = jnp.concatenate(hid, axis=1)
        mem = jnp.concatenate(mem, axis=1)
        hidden[s] = hid
        member[s] = mem
        return total + mm_nt(mem, jnp.concatenate([hid, jnp.ones_like(hid)], axis=0))

    sums = lax.fori_loop(0, fr // STEP, forward_step, jnp.zeros((anchors, LANES), F32))
    counts = sums[:, 64:]
    pooled = sums[:, :64] / counts
    head = w_head[...]
    project = mm_high(pooled, head)
    length = jnp.sqrt(jnp.sum(project * project, axis=1, keepdims=True) + EPS)
    embed = project / length
    short = pooled / length
    keys[pl.ds(date, 1)] = fold(short)[None]
    sends = [copy(keys.at[date], keys.at[date], s_key.at[o], r_key.at[date], dev) for o, dev in peers]
    for c in sends:
        c.start()
    back = mm_nt(embed, head, HIGH)
    for o, dev in peers:
        copy(keys.at[o], keys.at[o], s_key.at[o], r_key.at[o], dev).wait_recv()
    target = key_date[date]
    key_short = unfold(keys[target])
    scores = mm_nt(key_short, back, HIGH) / TEMP
    same = lax.broadcasted_iota(jnp.int32, (anchors, anchors), 0) == lax.broadcasted_iota(
        jnp.int32, (anchors, anchors), 1
    )
    positive = jnp.sum(jnp.where(same, scores, 0.0), axis=0, keepdims=True)
    weights = count_t[...] * jnp.exp(scores)
    exp_pos = jnp.exp(positive)
    denominator = exp_pos + jnp.sum(weights, axis=0, keepdims=True)
    scale = 1.0 / math.sqrt(dates * anchors * n_mem)
    d_scores = (scale / TEMP) * (
        weights / denominator + jnp.where(same, exp_pos / denominator - 1.0, 0.0)
    )
    grads[pl.ds(date, 1)] = fold(mm_high(d_scores, short))[None]
    more = [copy(grads.at[date], grads.at[date], s_gra.at[o], r_gra.at[date], dev) for o, dev in peers]
    for c in more:
        c.start()
    grad_short = mm_tn(d_scores, key_short, HIGH)
    losses = jnp.log(denominator) - positive
    n_down, n_across = fr // CELL, fc // CELL
    wide = n_across * tiles
    spot = lax.broadcasted_iota(jnp.int32, (wide, anchors), 1)
    pick = jnp.where(lax.rem(spot, wide) == lax.broadcasted_iota(jnp.int32, (wide, anchors), 0), losses, 0.0)
    line = lax.broadcasted_iota(jnp.int32, (n_down, anchors), 1) // wide
    lines = (line == lax.broadcasted_iota(jnp.int32, (n_down, anchors), 0)).astype(F32)
    loss_out[...] = mm_nt(pick, lines, HIGH).reshape(n_across, tiles, n_down)
    for o, dev in peers:
        copy(grads.at[o], grads.at[o], s_gra.at[o], r_gra.at[o], dev).wait_recv()
    returned = jnp.zeros(grads.shape[1:], F32)
    for d in range(dates):
        returned += jnp.where(key_date[d] == date, grads[d], 0.0)
    grad_embed = mm_high(grad_short + unfold(returned), head)
    grad_project = (
        grad_embed - embed * jnp.sum(embed * grad_embed, axis=1, keepdims=True)
    ) / length
    head_term = mm_tn(pooled, grad_project, HIGH)
    per_cell = (mm_nt(grad_project, head, HIGH) / counts).astype(BF)
    eye_c = (
        lax.broadcasted_iota(jnp.int32, (64, 64), 0) == lax.broadcasted_iota(jnp.int32, (64, 64), 1)
    ).astype(F32).astype(BF)
    cell_t = mm_nt(eye_c, per_cell).astype(BF)

    g_acc[...] = jnp.zeros_like(g_acc)

    def backward_step(s, carry):
        spread = mm(cell_t, member[s])
        slope = jnp.where(hidden[s].astype(F32) > 0.0, spread, 0.0)
        moved = [slope.astype(BF)]
        for b in range(1, 4):
            moved.append(
                jnp.concatenate(
                    [pltpu.roll(slope[:, r * LANES : (r + 1) * LANES], b, 1) for r in range(STEP)],
                    axis=1,
                ).astype(BF)
            )
        g_acc[...] += mm_nt(jnp.concatenate(moved, axis=0), wide_rows(s))
        return carry

    lax.fori_loop(0, fr // STEP, backward_step, 0)

    gr, hr = 256 // n_mem, 64 // n_mem
    for m in range(n_mem):
        part[m, :gr] = g_acc[m * gr : (m + 1) * gr].astype(BF)
        part[m, gr:] = jnp.concatenate([head_term[m * hr : (m + 1) * hr]] * 2, axis=1).astype(BF)
    sends += more
    gather1[pl.ds(me, 1)] = part[pl.ds(me, 1)]
    step1 = [copy(part.at[o], gather1.at[me], s_1.at[o], r_1.at[me], dev) for o, dev in members]
    for c in step1:
        c.start()
    for o, dev in members:
        copy(part.at[o], gather1.at[o], s_1.at[o], r_1.at[o], dev).wait_recv()
    total = gather1[0].astype(F32)
    for m in range(1, n_mem):
        total += gather1[m].astype(F32)
    gather2[pl.ds(date, 1)] = total.astype(BF)[None]
    step2 = [copy(gather2.at[date], gather2.at[date], s_2.at[o], r_2.at[date], dev) for o, dev in peers]
    for c in step2:
        c.start()
    for o, dev in peers:
        copy(gather2.at[o], gather2.at[o], s_2.at[o], r_2.at[o], dev).wait_recv()
    total = gather2[0].astype(F32)
    for d in range(1, dates):
        total += gather2[d].astype(F32)
    gather3[pl.ds(me, 1)] = total.astype(BF)[None]
    step3 = [copy(gather3.at[me], gather3.at[me], s_3.at[o], r_3.at[me], dev) for o, dev in members]
    for c in step3:
        c.start()
    for o, dev in members:
        copy(gather3.at[o], gather3.at[o], s_3.at[o], r_3.at[o], dev).wait_recv()
    for m in range(n_mem):
        head_out[m * hr : (m + 1) * hr] = gather3[m, gr:, :LANES].astype(F32)
    result = jnp.zeros((bands * 56, 64), F32)
    whole = jnp.concatenate([gather3[m, :gr] for m in range(n_mem)], axis=0)
    for b in range(4):
        result += mm_nt(taps[b], whole[64 * b : 64 * b + 64])
    stem_out[...] = result.reshape(bands, 7, 8, 64)[:, :, :7, :]

    for c in sends + step1 + step2 + step3:
        c.wait_send()

    @pl.when(col < n_col - 1)
    def _():
        to_right.wait_send()

    @pl.when(col > 0)
    def _():
        to_left.wait_send()

    @pl.when(row < n_row - 1)
    def _():
        down.wait_send()

    @pl.when(row > 0)
    def _():
        up.wait_send()


def solution(mesh):
    n_row, n_col, dates = mesh.shape["row"], mesh.shape["col"], mesh.shape["date"]

    def local(pixels, w_stem, w_head, pool_grid, neg_index, key_date):
        _, tiles, bands, height, width = pixels.shape
        fr, fc = height // 2, width // 2
        cells = fr // CELL * (fc // CELL)
        anchors = tiles * cells
        n_mem = n_row * n_col
        chunk = (256 + 64) // n_mem
        w_taps = jnp.pad(jnp.transpose(w_stem, (1, 2, 3, 0)), ((0, 0), (0, 0), (0, 1), (0, 0)))
        w_taps = w_taps.reshape(bands * 56, 64)
        grid_t = pool_grid.T
        neg = jnp.transpose(neg_index[0], (1, 2, 0, 3)).reshape(anchors, -1)
        place = np.zeros((fc, LANES), np.float32)
        for j in range(fc):
            for t in range(tiles):
                place[j, t * HALF + j] = 1
        vmem = pl.BlockSpec(memory_space=pltpu.VMEM)
        dma = pltpu.SemaphoreType.DMA
        cols, edge, halo, rows, taps = tables(tiles, bands, height, width)
        operands = (
            pixels[0], edge, w_taps, taps, grid_t, jnp.asarray(place, BF), neg, cols, halo, rows,
            w_head, key_date,
        )
        loss, stem, head = pl.pallas_call(
            functools.partial(kernel, (tiles, bands, height, width, n_row, n_col, dates)),
            out_shape=(
                jax.ShapeDtypeStruct((fc // CELL, tiles, fr // CELL), F32),
                jax.ShapeDtypeStruct((bands, 7, 7, 64), F32),
                jax.ShapeDtypeStruct((64, LANES), F32),
            ),
            in_specs=[pl.BlockSpec(memory_space=pltpu.HBM)] * len(operands),
            out_specs=(vmem, vmem, vmem),
            scratch_shapes=[pltpu.VMEM(x.shape, x.dtype) for x in operands[:-1]]
            + [pltpu.SMEM(key_date.shape, key_date.dtype)]
            + [
                pltpu.VMEM((2, bands, 16, height), BF),
                pltpu.VMEM((2, bands, 16, height), BF),
                pltpu.VMEM((height // 16 + 2, bands, 16, 2 * LANES), BF),
                pltpu.VMEM((height // 2 + 8, 2, 2, 16, LANES), BF),
                pltpu.VMEM((256, 256), BF),
                pltpu.VMEM((fr, LANES), F32),
                pltpu.VMEM((neg.shape[1], anchors), F32),
                pltpu.VMEM((anchors, anchors), F32),
                pltpu.VMEM((fr // STEP, anchors, STEP * LANES), BF),
                pltpu.VMEM((fr // STEP, 64, STEP * LANES), BF),
                pltpu.VMEM((dates, anchors // 2, LANES), F32),
                pltpu.VMEM((dates, anchors // 2, LANES), F32),
                pltpu.VMEM((256, 256), F32),
                pltpu.VMEM((n_mem, chunk, 256), BF),
                pltpu.VMEM((n_mem, chunk, 256), BF),
                pltpu.VMEM((dates, chunk, 256), BF),
                pltpu.VMEM((n_mem, chunk, 256), BF),
                dma((2,)), dma((2,)), dma((2,)), dma((2,)),
                dma((dates,)), dma((dates,)), dma((dates,)), dma((dates,)),
                dma((n_mem,)), dma((n_mem,)), dma((dates,)), dma((dates,)),
                dma((n_mem,)), dma((n_mem,)), dma((len(operands),)),
            ],
            compiler_params=pltpu.CompilerParams(
                collective_id=0, has_side_effects=True, vmem_limit_bytes=60 * 2**20
            ),
        )(*operands)
        loss = loss.transpose(1, 2, 0)[None]
        return loss, jnp.transpose(stem, (3, 0, 1, 2)), head

    return jax.shard_map(
        local,
        mesh=mesh,
        in_specs=(
            P(("groups", "date"), None, None, "row", "col"),
            P(),
            P(),
            P("row", "col"),
            P(("groups", "date"), None, "row", "col", None),
            P(),
        ),
        out_specs=(
            P(("groups", "date"), None, "row", "col"),
            P("groups", None, None, None),
            P("groups", None),
        ),
        check_vma=False,
    )
```
